32 devices in a mesh: prompt: 4 (over y, x), sample: 8 (over z, core).
Axes of the slice: x: 2, y: 2, z: 4, core: 2. Of those that a mesh axis runs over, the one named last changes fastest.
Arguments:
- embeddings: bfloat16 [32, 512, 1024], P(('prompt', 'sample')), parts along dimension 0
- lengths: int32 [32], P(('prompt', 'sample')), parts along dimension 0, may hold values from 32 to 512, as said below
Outputs:
- precision: float32 [32, 8], P(('prompt', 'sample')), parts along dimension 0
- utility: float32 [32], P(('prompt', 'sample')), parts along dimension 0
The draws below stay inside these ranges and needn't reach their ends.
There are 4 independent parts, one for each index of `prompt`. The reference program is written for one: setup_inputs(seed, part) draws one part's arguments, and reference() takes and returns one part's arrays. A program takes and returns all parts, laid end to end along the dimension named above; each array names one. Nothing has to cross between parts.
Inputs may be any that keep to these rules, and one draw needn't show every extreme that they name: `lengths`: some sample of the prompt has exactly 512 tokens.
All inputs are finite; a program needn't handle non-finite values.
Results may differ from the reference program's by a relative error of at most 0.0007.
Values may be sent and summed in bfloat16 or wider, within the bound.
A program may use at most 128 MiB of HBM per device.

```python
import jax
import jax.numpy as jnp
from jax import lax

E = 1024
LEN = 512
SAMPLES = 8


def draw_embeddings(key, part):
    keys = jax.random.split(jax.random.fold_in(key, 11), 4)
    pool = jax.random.normal(keys[0], (256, E), jnp.float32)
    offset = jax.random.randint(keys[1], (SAMPLES, 1), 0, 160)
    concept = offset + jax.random.randint(keys[2], (SAMPLES, LEN), 0, 96)
    centre = jnp.take(pool, concept, axis=0)
    noise = jax.random.normal(keys[3], (SAMPLES, LEN, E), jnp.float32)
    result = centre + 0.6 * noise
    return result.astype(jnp.bfloat16)


def draw_lengths(key, part):
    keys = jax.random.split(jax.random.fold_in(key, 23), 2)
    drawn = jax.random.randint(keys[0], (SAMPLES,), max(1, LEN // 16), LEN + 1)
    chosen = jax.random.randint(keys[1], (), 0, SAMPLES)
    return jnp.where(jnp.arange(SAMPLES) == chosen, LEN, drawn).astype(jnp.int32)


def setup_inputs(seed: int = 0, part: int = 0) -> dict:
    arg_keys = jax.random.split(jax.random.key(seed), 3)
    part_splits = jax.random.split(jax.random.fold_in(arg_keys[2], part), 3)
    return {
        "embeddings": draw_embeddings(jax.random.fold_in(jax.random.fold_in(arg_keys[2], part), 71), part),
        "lengths": draw_lengths(jax.random.fold_in(jax.random.fold_in(arg_keys[2], part), 71), part),
    }


def reference(embeddings, lengths):
    values = embeddings.astype(jnp.float32)
    unit = (values / jnp.sqrt(lax.optimization_barrier(jnp.sum(values * values, axis=2, keepdims=True)) + 1e-06)).astype(jnp.bfloat16)
    flat = unit.reshape(SAMPLES * LEN, E)
    places = jnp.arange(LEN, dtype=jnp.int32)
    valid = places[None, :] < lengths[:, None]

    def one_row(items):
        own, own_len = items
        similar = jnp.dot(own, flat.T, preferred_element_type=jnp.float32).reshape(LEN, SAMPLES, LEN)
        masked = jnp.where(valid[None, :, :], similar, jnp.float32(-4.0))
        best = lax.optimization_barrier(jnp.max(masked, axis=2))
        keep = places[:, None] < own_len
        return lax.optimization_barrier(jnp.sum(jnp.where(keep, best, jnp.float32(0.0)), axis=0)) / own_len.astype(jnp.float32)
    precision = lax.map(one_row, (unit, lengths))
    both = precision + precision.T
    offdiag = jnp.arange(SAMPLES)[:, None] != jnp.arange(SAMPLES)[None, :]
    utility = lax.optimization_barrier(jnp.sum(jnp.where(offdiag, both, jnp.float32(0.0)), axis=1)) / jnp.float32(2 * (SAMPLES - 1))
    return (precision, utility)
```

```python
import functools

import jax
import jax.numpy as jnp
from jax import lax
from jax.experimental import pallas as pl
from jax.experimental.pallas import tpu as pltpu
from jax.sharding import PartitionSpec as P

MESH = pl.DeviceIdType.MESH
LOW = -4.0
T = 128


def kernel(chips, slots, len_ref, emb_ref, prec_ref, util_ref, units, relay, lens, rows, cols, res,
           unit_in, relay_in, lens_in, res_in, send, side, pass_on, lens_out, res_out):
    p, s = lax.axis_index("prompt"), lax.axis_index("sample")
    x, y, z, c = p % 2, p // 2, s // 2, s % 2
    flip = (x + y) % 2
    hub_z = jnp.where(flip == 0, 2, 1)
    v = jnp.where(flip == 0, z, chips - 1 - z)
    across = jnp.where(c == 0, p + 1 - 2 * x, p + 2 - 4 * y)
    chunks = units.shape[0]
    is_hub = v == 2
    is_near = v == 1
    f32 = jnp.float32

    def at(prompt, sample):
        return {"prompt": prompt, "sample": sample}

    def copy(src, dst, out_sem, in_sem, where):
        return pltpu.make_async_remote_copy(
            src_ref=src, dst_ref=dst, send_sem=out_sem, recv_sem=in_sem,
            device_id=where, device_id_type=MESH)

    barrier = pltpu.get_barrier_semaphore()

    def greet(prompt, sample):
        pl.semaphore_signal(barrier, inc=1, device_id=at(prompt, sample), device_id_type=MESH)

    @pl.when(is_hub)
    def _():
        for d in range(1, slots):
            greet(p, lax.rem(s + d, slots))
        greet(across, s)
        greet(across, 2 * (chips - 1 - z) + c)

    @pl.when(jnp.logical_not(is_hub))
    def _():
        greet(p, 2 * hub_z)
        greet(p, 2 * hub_z + 1)

    @pl.when(is_near)
    def _():
        greet(across, s)

    lens[s] = jnp.full(lens.shape[1:], len_ref[0], jnp.int32)

    @pl.loop(0, chunks)
    def _(k):
        values = emb_ref[0, pl.ds(pl.multiple_of(k * T, T), T), :].astype(f32)
        norm = jnp.sqrt(jnp.sum(values * values, axis=1, keepdims=True) + 1e-06)
        units[k, s] = (values / norm).astype(units.dtype)

    @pl.when(is_hub)
    def _():
        rows[...] = jnp.full(rows.shape, LOW, f32)
        cols[...] = jnp.full(cols.shape, LOW, f32)
        pl.semaphore_wait(barrier, slots + 1)

    @pl.when(is_near)
    def _():
        pl.semaphore_wait(barrier, 3)

    @pl.when(jnp.logical_not(is_hub | is_near))
    def _():
        pl.semaphore_wait(barrier, 2)

    def own(k):
        return units.at[k, s]

    def straight(k):
        return copy(own(k), own(k), send.at[k], unit_in.at[s, k], at(p, 2 * hub_z + c))

    def detour(k):
        return copy(own(k), relay.at[k], send.at[k], relay_in.at[k], at(across, s))

    def hand_on(k):
        return copy(relay.at[k], units.at[k, s], pass_on.at[k], unit_in.at[s, k],
                    at(across, 2 * (chips - 1 - z) + c))

    def to_side(k, slot):
        return copy(units.at[k, slot], units.at[k, slot], side.at[slot, k], unit_in.at[slot, k],
                    at(p, 2 * z + 1 - c))

    def tell(core, where):
        return copy(lens.at[s], lens.at[s], lens_out.at[core], lens_in.at[s], where)

    far = jnp.logical_not(is_hub | is_near)

    @pl.when(far)
    def _():
        for k in range(chunks):
            straight(k).start()

    @pl.when(is_near)
    def _():
        for k in range(chunks):
            detour(k).start()

    @pl.when(jnp.logical_not(is_hub))
    def _():
        for core in range(2):
            tell(core, at(p, 2 * hub_z + core)).start()

    @pl.when(is_hub)
    def _():
        tell(0, at(p, 2 * z + 1 - c)).start()
        for k in range(chunks):
            to_side(k, s).start()

        def step(k):
            return 2 * lax.rem(z + k, chips)

        def others(k):
            return [step(d) + c for d in range(1, chips)]

        hand_wait = lambda k: copy(relay.at[k], relay.at[k], pass_on.at[k], relay_in.at[k],
                                   at(p, 2 * z + 1 - c)).wait_recv()
        hand_wait(0)
        hand_on(0).start()
        for d in range(1, slots):
            other = lax.rem(s + d, slots)
            copy(lens.at[other], lens.at[other], lens_out.at[0], lens_in.at[other],
                 at(p, 2 * z + 1 - c)).wait_recv()

        lane = lax.broadcasted_iota(jnp.int32, (1, T), 1)
        lane8 = lax.broadcasted_iota(jnp.int32, (T, T), 1)
        sub = lax.broadcasted_iota(jnp.int32, (T, T), 0)
        high = f32(4.0)

        def col_cap(k, slot):
            return jnp.where(lane + k * T < lens[slot, 0:1, :], high, f32(LOW))

        def row_cap(k, slot):
            return jnp.where(sub + k * T < lens[slot, 0:1, :], high, f32(LOW))

        def group(k, g):
            return units[k, pl.ds(2 * g, 2)].reshape(2 * T, units.shape[3])

        def against(k, g, h, js, keep):
            new = group(k, g)
            best = [[None, None], [None, None]]
            caps = [row_cap(k, 2 * g + q) for q in range(2)]
            for j in js:
                similar = lax.dot_general(new, group(j, h), (((1,), (1,)), ((), ())),
                                          preferred_element_type=f32)
                for w in range(2):
                    cap = col_cap(j, 2 * h + w)
                    for q in range(2):
                        part = similar[q * T:(q + 1) * T, w * T:(w + 1) * T]
                        m = jnp.minimum(part, cap)
                        best[q][w] = m if best[q][w] is None else jnp.maximum(best[q][w], m)
                        if keep(j):
                            n = jnp.max(jnp.minimum(part, caps[q]), axis=0, keepdims=True)
                            at_row = (2 * h + w) * slots + 2 * g + q
                            cols[j, pl.ds(at_row, 1), :] = jnp.maximum(cols[j, pl.ds(at_row, 1), :], n)
            table = rows[k]
            for q in range(2):
                for w in range(2):
                    top = jnp.max(best[q][w], axis=1, keepdims=True)
                    table = jnp.where(lane8 == (2 * g + q) * slots + 2 * h + w, top, table)
            rows[k] = table

        for k in range(chunks):
            if k + 1 < chunks:
                hand_wait(k + 1)
                hand_on(k + 1).start()
            for slot in others(k):
                to_side(k, slot).wait_recv()
                to_side(k, slot).start()
            for d in range(chips):
                to_side(k, step(d) + 1 - c).wait_recv()

            @pl.loop(0, chips - 1)
            def _(i):
                g = jnp.where(c == 0, i, lax.rem(3 * i + 2, chips + 1))
                h = jnp.where(c == 0, i + 1, lax.rem(3 * i + 5, chips + 1))
                against(k, g, h, range(k + 1), lambda j: True)
                if k:
                    against(k, h, g, range(k), lambda j: True)

            @pl.loop(0, 2)
            def _(i):
                g = 2 * c + i
                against(k, g, g, range(k + 1), lambda j: j < k)

        pair = slots * slots
        total = jnp.zeros((pair, 1), f32)
        own_len = jnp.concatenate([lens[a] for a in range(slots)], axis=0)
        for k in range(chunks):
            best = jnp.maximum(rows[k].T[:pair], cols[k, :pair])
            ok = (lax.broadcasted_iota(jnp.int32, (pair, T), 1) + k * T < own_len) & (best > -3.5)
            total += jnp.sum(jnp.where(ok, best, f32(0.0)), axis=1, keepdims=True)
        res[c] = total / own_len.astype(f32)
        for d in range(1, slots):
            copy(res.at[c], res.at[c], res_out.at[d], res_in.at[c], at(p, lax.rem(s + d, slots))).start()
        for k in range(chunks):
            hand_on(k).wait_send()
            for d in range(chips):
                to_side(k, step(d) + c).wait_send()
        tell(0, at(p, 2 * z + 1 - c)).wait_send()
        copy(res.at[1 - c], res.at[1 - c], res_out.at[0], res_in.at[1 - c], at(p, 2 * z + 1 - c)).wait_recv()

    @pl.when(jnp.logical_not(is_hub))
    def _():
        for k in range(chunks):
            straight(k).wait_send()
        for core in range(2):
            tell(core, at(p, 2 * hub_z + core)).wait_send()
        for core in range(2):
            copy(res.at[core], res.at[core], res_out.at[0], res_in.at[core],
                 at(p, 2 * hub_z + core)).wait_recv()

    whole = res[0] + res[1]
    pair = slots * slots
    index = lax.broadcasted_iota(jnp.int32, (pair, T), 0)
    lanes = lax.broadcasted_iota(jnp.int32, (pair, T), 1)
    row = jnp.sum(jnp.where(index == s * slots + lanes, whole, f32(0.0)), axis=0, keepdims=True)
    prec_ref[...] = row[:, :slots]
    first, second = index // slots, index % slots
    mine = ((first == s) | (second == s)) & (first != second)
    both = jnp.sum(jnp.where(mine, whole, f32(0.0)), axis=0, keepdims=True) / f32(2 * (slots - 1))
    util_ref[...] = both[:, :1]

    @pl.when(is_hub)
    def _():
        for d in range(1, slots):
            copy(res.at[c], res.at[c], res_out.at[d], res_in.at[c], at(p, lax.rem(s + d, slots))).wait_send()


def fused(slots, embeddings, lengths):
    length, width = embeddings.shape[1:]
    chunks = length // T
    dma = pltpu.SemaphoreType.DMA
    precision, utility = pl.pallas_call(
        functools.partial(kernel, slots // 2, slots),
        out_shape=(jax.ShapeDtypeStruct((1, slots), jnp.float32), jax.ShapeDtypeStruct((1, 1), jnp.float32)),
        in_specs=[pl.BlockSpec(memory_space=pltpu.SMEM), pl.BlockSpec(memory_space=pltpu.VMEM)],
        out_specs=(pl.BlockSpec(memory_space=pltpu.VMEM), pl.BlockSpec(memory_space=pltpu.VMEM)),
        scratch_shapes=[
            pltpu.VMEM((chunks, slots, T, width), jnp.bfloat16),
            pltpu.VMEM((chunks, T, width), jnp.bfloat16),
            pltpu.VMEM((slots, 8, T), jnp.int32),
            pltpu.VMEM((chunks, T, T), jnp.float32),
            pltpu.VMEM((chunks, slots * slots, T), jnp.float32),
            pltpu.VMEM((2, slots * slots, T), jnp.float32),
            dma((slots, chunks)), dma((chunks,)), dma((slots,)), dma((2,)),
            dma((chunks,)), dma((slots, chunks)), dma((chunks,)), dma((2,)), dma((slots,)),
        ],
        compiler_params=pltpu.CompilerParams(collective_id=0, has_side_effects=True),
    )(lengths, embeddings)
    return precision, utility[:, 0]


def tile_pairs(own, own_len, other, other_len):
    similar = jnp.einsum("aie,bje->abij", own, other, preferred_element_type=jnp.float32)
    places = jnp.arange(own.shape[1], dtype=jnp.int32)
    own_ok = places[None, :] < own_len[:, None]
    other_ok = places[None, :] < other_len[:, None]
    masked = jnp.where(other_ok[None, :, None, :], similar, jnp.float32(-4.0))
    best_row = jnp.max(masked, axis=3)
    forward = jnp.sum(jnp.where(own_ok[:, None, :], best_row, jnp.float32(0.0)), axis=2)
    forward = forward / own_len[:, None].astype(jnp.float32)
    masked_col = jnp.where(own_ok[:, None, :, None], similar, jnp.float32(-4.0))
    best_col = jnp.max(masked_col, axis=2)
    backward = jnp.sum(jnp.where(other_ok[None, :, :], best_col, jnp.float32(0.0)), axis=2)
    backward = backward / other_len[None, :].astype(jnp.float32)
    return (forward, backward)


def body(embeddings, lengths):
    values = embeddings.astype(jnp.float32)
    unit = (values / jnp.sqrt(jnp.sum(values * values, axis=2, keepdims=True) + 1e-06)).astype(
        jnp.bfloat16
    )
    devices = lax.axis_size("sample")
    here = lax.axis_index("sample")
    per_dev = unit.shape[0]
    total = per_dev * devices
    base = here * per_dev
    piece = lax.all_gather(unit, "sample", axis=0, tiled=True)
    piece_len = lax.all_gather(lengths, "sample", axis=0, tiled=True)
    ahead, behind = tile_pairs(unit, lengths, piece, piece_len)
    own_index = base + jnp.arange(per_dev, dtype=jnp.int32)
    offdiag = jnp.arange(total, dtype=jnp.int32)[None, :] != own_index[:, None]
    utility = jnp.sum(jnp.where(offdiag, ahead + behind, jnp.float32(0.0)), axis=1)
    utility = utility / jnp.float32(2 * (total - 1))
    return (ahead, utility)


def solution(mesh):
    in_specs = (P(("prompt", "sample"), None, None), P(("prompt", "sample")))
    out_specs = (P(("prompt", "sample"), None), P(("prompt", "sample")))

    def run(embeddings, lengths):
        slots = mesh.shape["sample"]
        if mesh.shape["prompt"] == 4 and slots == 8 and embeddings.shape[0] == 1 and embeddings.shape[1] % T == 0:
            return fused(slots, embeddings, lengths)
        return body(embeddings, lengths)

    return jax.shard_map(run, mesh=mesh, in_specs=in_specs, out_specs=out_specs, check_vma=False)
```

```python
import functools

import jax
import jax.numpy as jnp
from jax import lax
from jax.experimental import pallas as pl
from jax.experimental.pallas import tpu as pltpu
from jax.sharding import PartitionSpec as P

MESH = pl.DeviceIdType.MESH
LOW = -4.0
T = 128


def kernel(chips, slots, len_ref, emb_ref, prec_ref, util_ref, units, relay, lens, rows, cols, res,
           unit_in, relay_in, lens_in, res_in, send, side, pass_on, lens_out, res_out):
    p, s = lax.axis_index("prompt"), lax.axis_index("sample")
    x, y, z, c = p % 2, p // 2, s // 2, s % 2
    flip = (x + y) % 2
    hub_z = jnp.where(flip == 0, 2, 1)
    v = jnp.where(flip == 0, z, chips - 1 - z)
    across = jnp.where(c == 0, p + 1 - 2 * x, p + 2 - 4 * y)
    chunks = units.shape[0]
    is_hub = v == 2
    is_near = v == 1
    f32 = jnp.float32

    def at(prompt, sample):
        return {"prompt": prompt, "sample": sample}

    def copy(src, dst, out_sem, in_sem, where):
        return pltpu.make_async_remote_copy(
            src_ref=src, dst_ref=dst, send_sem=out_sem, recv_sem=in_sem,
            device_id=where, device_id_type=MESH)

    barrier = pltpu.get_barrier_semaphore()

    def greet(prompt, sample):
        pl.semaphore_signal(barrier, inc=1, device_id=at(prompt, sample), device_id_type=MESH)

    @pl.when(is_hub)
    def _():
        for d in range(1, slots):
            greet(p, lax.rem(s + d, slots))
        greet(across, s)
        greet(across, 2 * (chips - 1 - z) + c)

    @pl.when(jnp.logical_not(is_hub))
    def _():
        greet(p, 2 * hub_z)
        greet(p, 2 * hub_z + 1)

    @pl.when(is_near)
    def _():
        greet(across, s)

    lens[s] = jnp.full(lens.shape[1:], len_ref[0], jnp.int32)

    @pl.loop(0, chunks)
    def _(k):
        values = emb_ref[0, pl.ds(pl.multiple_of(k * T, T), T), :].astype(f32)
        norm = jnp.sqrt(jnp.sum(values * values, axis=1, keepdims=True) + 1e-06)
        units[k, s] = (values / norm).astype(units.dtype)

    @pl.when(is_hub)
    def _():
        rows[...] = jnp.full(rows.shape, LOW, f32)
        cols[...] = jnp.full(cols.shape, LOW, f32)
        pl.semaphore_wait(barrier, slots + 1)

    @pl.when(is_near)
    def _():
        pl.semaphore_wait(barrier, 3)

    @pl.when(jnp.logical_not(is_hub | is_near))
    def _():
        pl.semaphore_wait(barrier, 2)

    def own(k):
        return units.at[k, s]

    def straight(k):
        return copy(own(k), own(k), send.at[k], unit_in.at[s, k], at(p, 2 * hub_z + c))

    def detour(k):
        return copy(own(k), relay.at[k], send.at[k], relay_in.at[k], at(across, s))

    def hand_on(k):
        return copy(relay.at[k], units.at[k, s], pass_on.at[k], unit_in.at[s, k],
                    at(across, 2 * (chips - 1 - z) + c))

    def to_side(k, slot):
        return copy(units.at[k, slot], units.at[k, slot], side.at[slot, k], unit_in.at[slot, k],
                    at(p, 2 * z + 1 - c))

    def tell(core, where):
        return copy(lens.at[s], lens.at[s], lens_out.at[core], lens_in.at[s], where)

    far = jnp.logical_not(is_hub | is_near)

    @pl.when(far)
    def _():
        for k in range(chunks):
            straight(k).start()

    @pl.when(is_near)
    def _():
        for k in range(chunks):
            detour(k).start()

    @pl.when(jnp.logical_not(is_hub))
    def _():
        for core in range(2):
            tell(core, at(p, 2 * hub_z + core)).start()

    @pl.when(is_hub)
    def _():
        tell(0, at(p, 2 * z + 1 - c)).start()
        for k in range(chunks):
            to_side(k, s).start()

        def step(k):
            return 2 * lax.rem(z + k, chips)

        def others(k):
            return [step(d) + c for d in range(1, chips)]

        hand_wait = lambda k: copy(relay.at[k], relay.at[k], pass_on.at[k], relay_in.at[k],
                                   at(p, 2 * z + 1 - c)).wait_recv()
        for k in range(3):
            hand_wait(k)
            hand_on(k).start()
        for d in range(1, slots):
            other = lax.rem(s + d, slots)
            copy(lens.at[other], lens.at[other], lens_out.at[0], lens_in.at[other],
                 at(p, 2 * z + 1 - c)).wait_recv()

        lane = lax.broadcasted_iota(jnp.int32, (1, T), 1)
        lane8 = lax.broadcasted_iota(jnp.int32, (T, T), 1)
        sub = lax.broadcasted_iota(jnp.int32, (T, T), 0)
        high = f32(4.0)

        def col_cap(k, slot):
            return jnp.where(lane + k * T < lens[slot, 0:1, :], high, f32(LOW))

        def row_cap(k, slot):
            return jnp.where(sub + k * T < lens[slot, 0:1, :], high, f32(LOW))

        def group(k, g):
            return units[k, pl.ds(2 * g, 2)].reshape(2 * T, units.shape[3])

        def against(k, g, h, js, keep):
            new = group(k, g)
            best = [[None, None], [None, None]]
            caps = [row_cap(k, 2 * g + q) for q in range(2)]
            for j in js:
                similar = lax.dot_general(new, group(j, h), (((1,), (1,)), ((), ())),
                                          preferred_element_type=f32)
                for w in range(2):
                    cap = col_cap(j, 2 * h + w)
                    for q in range(2):
                        part = similar[q * T:(q + 1) * T, w * T:(w + 1) * T]
                        m = jnp.minimum(part, cap)
                        best[q][w] = m if best[q][w] is None else jnp.maximum(best[q][w], m)
                        if keep(j):
                            n = jnp.max(jnp.minimum(part, caps[q]), axis=0, keepdims=True)
                            at_row = (2 * h + w) * slots + 2 * g + q
                            cols[j, pl.ds(at_row, 1), :] = jnp.maximum(cols[j, pl.ds(at_row, 1), :], n)
            table = rows[k]
            for q in range(2):
                for w in range(2):
                    top = jnp.max(best[q][w], axis=1, keepdims=True)
                    table = jnp.where(lane8 == (2 * g + q) * slots + 2 * h + w, top, table)
            rows[k] = table

        for k in range(chunks):
            if k + 3 < chunks:
                hand_wait(k + 3)
                hand_on(k + 3).start()
            for slot in others(k):
                to_side(k, slot).wait_recv()
                to_side(k, slot).start()
            for d in range(chips):
                to_side(k, step(d) + 1 - c).wait_recv()

            @pl.loop(0, chips - 1, unroll=True)
            def _(i):
                g = jnp.where(c == 0, i, lax.rem(3 * i + 2, chips + 1))
                h = jnp.where(c == 0, i + 1, lax.rem(3 * i + 5, chips + 1))
                against(k, g, h, range(k + 1), lambda j: True)
                if k:
                    against(k, h, g, range(k), lambda j: True)

            @pl.loop(0, 2, unroll=True)
            def _(i):
                g = 2 * c + i
                against(k, g, g, range(k + 1), lambda j: j < k)

        pair = slots * slots
        total = jnp.zeros((pair, 1), f32)
        own_len = jnp.concatenate([lens[a] for a in range(slots)], axis=0)
        for k in range(chunks):
            best = jnp.maximum(rows[k].T[:pair], cols[k, :pair])
            ok = (lax.broadcasted_iota(jnp.int32, (pair, T), 1) + k * T < own_len) & (best > -3.5)
            total += jnp.sum(jnp.where(ok, best, f32(0.0)), axis=1, keepdims=True)
        share = total / own_len.astype(f32)
        place = lax.broadcasted_iota(jnp.int32, (pair, T), 0) % slots
        spread = jnp.where(lax.broadcasted_iota(jnp.int32, (pair, T), 1) == place, share, f32(0.0))
        res[c] = jnp.sum(spread.reshape(slots, slots, T), axis=1)
        for d in range(1, slots):
            copy(res.at[c], res.at[c], res_out.at[d], res_in.at[c], at(p, lax.rem(s + d, slots))).start()
        for k in range(chunks):
            hand_on(k).wait_send()
            for d in range(chips):
                to_side(k, step(d) + c).wait_send()
        tell(0, at(p, 2 * z + 1 - c)).wait_send()
        copy(res.at[1 - c], res.at[1 - c], res_out.at[0], res_in.at[1 - c], at(p, 2 * z + 1 - c)).wait_recv()

    @pl.when(jnp.logical_not(is_hub))
    def _():
        for k in range(chunks):
            straight(k).wait_send()
        for core in range(2):
            tell(core, at(p, 2 * hub_z + core)).wait_send()
        for core in range(2):
            copy(res.at[core], res.at[core], res_out.at[0], res_in.at[core],
                 at(p, 2 * hub_z + core)).wait_recv()

    whole = res[0] + res[1]
    first = lax.broadcasted_iota(jnp.int32, (slots, T), 0)
    second = lax.broadcasted_iota(jnp.int32, (slots, T), 1)
    row = jnp.sum(jnp.where(first == s, whole, f32(0.0)), axis=0, keepdims=True)
    prec_ref[...] = row[:, :slots]
    mine = ((first == s) | (second == s)) & (first != second)
    both = jnp.sum(jnp.where(mine, whole, f32(0.0)), axis=0, keepdims=True)
    util_ref[...] = jnp.sum(both, axis=1, keepdims=True) / f32(2 * (slots - 1))

    @pl.when(is_hub)
    def _():
        for d in range(1, slots):
            copy(res.at[c], res.at[c], res_out.at[d], res_in.at[c], at(p, lax.rem(s + d, slots))).wait_send()


def fused(slots, embeddings, lengths):
    length, width = embeddings.shape[1:]
    chunks = length // T
    dma = pltpu.SemaphoreType.DMA
    precision, utility = pl.pallas_call(
        functools.partial(kernel, slots // 2, slots),
        out_shape=(jax.ShapeDtypeStruct((1, slots), jnp.float32), jax.ShapeDtypeStruct((1, 1), jnp.float32)),
        in_specs=[pl.BlockSpec(memory_space=pltpu.SMEM), pl.BlockSpec(memory_space=pltpu.VMEM)],
        out_specs=(pl.BlockSpec(memory_space=pltpu.VMEM), pl.BlockSpec(memory_space=pltpu.VMEM)),
        scratch_shapes=[
            pltpu.VMEM((chunks, slots, T, width), jnp.bfloat16),
            pltpu.VMEM((chunks, T, width), jnp.bfloat16),
            pltpu.VMEM((slots, 8, T), jnp.int32),
            pltpu.VMEM((chunks, T, T), jnp.float32),
            pltpu.VMEM((chunks, slots * slots, T), jnp.float32),
            pltpu.VMEM((2, slots, T), jnp.float32),
            dma((slots, chunks)), dma((chunks,)), dma((slots,)), dma((2,)),
            dma((chunks,)), dma((slots, chunks)), dma((chunks,)), dma((2,)), dma((slots,)),
        ],
        compiler_params=pltpu.CompilerParams(collective_id=0, has_side_effects=True),
    )(lengths, embeddings)
    return precision, utility[:, 0]


def tile_pairs(own, own_len, other, other_len):
    similar = jnp.einsum("aie,bje->abij", own, other, preferred_element_type=jnp.float32)
    places = jnp.arange(own.shape[1], dtype=jnp.int32)
    own_ok = places[None, :] < own_len[:, None]
    other_ok = places[None, :] < other_len[:, None]
    masked = jnp.where(other_ok[None, :, None, :], similar, jnp.float32(-4.0))
    best_row = jnp.max(masked, axis=3)
    forward = jnp.sum(jnp.where(own_ok[:, None, :], best_row, jnp.float32(0.0)), axis=2)
    forward = forward / own_len[:, None].astype(jnp.float32)
    masked_col = jnp.where(own_ok[:, None, :, None], similar, jnp.float32(-4.0))
    best_col = jnp.max(masked_col, axis=2)
    backward = jnp.sum(jnp.where(other_ok[None, :, :], best_col, jnp.float32(0.0)), axis=2)
    backward = backward / other_len[None, :].astype(jnp.float32)
    return (forward, backward)


def body(embeddings, lengths):
    values = embeddings.astype(jnp.float32)
    unit = (values / jnp.sqrt(jnp.sum(values * values, axis=2, keepdims=True) + 1e-06)).astype(
        jnp.bfloat16
    )
    devices = lax.axis_size("sample")
    here = lax.axis_index("sample")
    per_dev = unit.shape[0]
    total = per_dev * devices
    base = here * per_dev
    piece = lax.all_gather(unit, "sample", axis=0, tiled=True)
    piece_len = lax.all_gather(lengths, "sample", axis=0, tiled=True)
    ahead, behind = tile_pairs(unit, lengths, piece, piece_len)
    own_index = base + jnp.arange(per_dev, dtype=jnp.int32)
    offdiag = jnp.arange(total, dtype=jnp.int32)[None, :] != own_index[:, None]
    utility = jnp.sum(jnp.where(offdiag, ahead + behind, jnp.float32(0.0)), axis=1)
    utility = utility / jnp.float32(2 * (total - 1))
    return (ahead, utility)


def solution(mesh):
    in_specs = (P(("prompt", "sample"), None, None), P(("prompt", "sample")))
    out_specs = (P(("prompt", "sample"), None), P(("prompt", "sample")))

    def run(embeddings, lengths):
        slots = mesh.shape["sample"]
        if mesh.shape["prompt"] == 4 and slots == 8 and embeddings.shape[0] == 1 and embeddings.shape[1] % T == 0:
            return fused(slots, embeddings, lengths)
        return body(embeddings, lengths)

    return jax.shard_map(run, mesh=mesh, in_specs=in_specs, out_specs=out_specs, check_vma=False)
```

```python
import functools

import jax
import jax.numpy as jnp
from jax import lax
from jax.experimental import pallas as pl
from jax.experimental.pallas import tpu as pltpu
from jax.sharding import PartitionSpec as P

MESH = pl.DeviceIdType.MESH
LOW = -4.0
T = 128


def kernel(chips, slots, len_ref, emb_ref, prec_ref, util_ref, units, relay, lens, rows, cols, res,
           unit_in, relay_in, lens_in, res_in, send, side, pass_on, lens_out, res_out):
    p, s = lax.axis_index("prompt"), lax.axis_index("sample")
    x, y, z, c = p % 2, p // 2, s // 2, s % 2
    flip = (x + y) % 2
    hub_z = jnp.where(flip == 0, 2, 1)
    v = jnp.where(flip == 0, z, chips - 1 - z)
    across = jnp.where(c == 0, p + 1 - 2 * x, p + 2 - 4 * y)
    chunks = units.shape[0]
    is_hub = v == 2
    is_near = v == 1
    f32 = jnp.float32

    def at(prompt, sample):
        return {"prompt": prompt, "sample": sample}

    def copy(src, dst, out_sem, in_sem, where):
        return pltpu.make_async_remote_copy(
            src_ref=src, dst_ref=dst, send_sem=out_sem, recv_sem=in_sem,
            device_id=where, device_id_type=MESH)

    barrier = pltpu.get_barrier_semaphore()

    def greet(prompt, sample):
        pl.semaphore_signal(barrier, inc=1, device_id=at(prompt, sample), device_id_type=MESH)

    @pl.when(is_hub)
    def _():
        for d in range(1, slots):
            greet(p, lax.rem(s + d, slots))
        greet(across, s)
        greet(across, 2 * (chips - 1 - z) + c)

    @pl.when(jnp.logical_not(is_hub))
    def _():
        greet(p, 2 * hub_z)
        greet(p, 2 * hub_z + 1)

    @pl.when(is_near)
    def _():
        greet(across, s)

    lens[s] = jnp.full(lens.shape[1:], len_ref[0], jnp.int32)

    @pl.loop(0, chunks)
    def _(k):
        values = emb_ref[0, pl.ds(pl.multiple_of(k * T, T), T), :].astype(f32)
        norm = jnp.sqrt(jnp.sum(values * values, axis=1, keepdims=True) + 1e-06)
        units[k, s] = (values / norm).astype(units.dtype)

    @pl.when(is_hub)
    def _():
        rows[...] = jnp.full(rows.shape, LOW, f32)
        cols[...] = jnp.full(cols.shape, LOW, f32)
        pl.semaphore_wait(barrier, slots + 1)

    @pl.when(is_near)
    def _():
        pl.semaphore_wait(barrier, 3)

    @pl.when(jnp.logical_not(is_hub | is_near))
    def _():
        pl.semaphore_wait(barrier, 2)

    def own(k):
        return units.at[k, s]

    def straight(k):
        return copy(own(k), own(k), send.at[k], unit_in.at[s, k], at(p, 2 * hub_z + c))

    def detour(k):
        return copy(own(k), relay.at[k], send.at[k], relay_in.at[k], at(across, s))

    def hand_on(k):
        return copy(relay.at[k], units.at[k, s], pass_on.at[k], unit_in.at[s, k],
                    at(across, 2 * (chips - 1 - z) + c))

    def to_side(k, slot):
        return copy(units.at[k, slot], units.at[k, slot], side.at[slot, k], unit_in.at[slot, k],
                    at(p, 2 * z + 1 - c))

    def tell(core, where):
        return copy(lens.at[s], lens.at[s], lens_out.at[core], lens_in.at[s], where)

    far = jnp.logical_not(is_hub | is_near)

    @pl.when(far)
    def _():
        for k in range(chunks):
            straight(k).start()

    @pl.when(is_near)
    def _():
        for k in range(chunks):
            detour(k).start()

    @pl.when(jnp.logical_not(is_hub))
    def _():
        for core in range(2):
            tell(core, at(p, 2 * hub_z + core)).start()

    @pl.when(is_hub)
    def _():
        tell(0, at(p, 2 * z + 1 - c)).start()
        for k in range(chunks):
            to_side(k, s).start()

        def step(k):
            return 2 * lax.rem(z + k, chips)

        def others(k):
            return [step(d) + c for d in range(1, chips)]

        hand_wait = lambda k: copy(relay.at[k], relay.at[k], pass_on.at[k], relay_in.at[k],
                                   at(p, 2 * z + 1 - c)).wait_recv()
        for k in range(chunks):
            hand_wait(k)
            hand_on(k).start()
        for d in range(1, slots):
            other = lax.rem(s + d, slots)
            copy(lens.at[other], lens.at[other], lens_out.at[0], lens_in.at[other],
                 at(p, 2 * z + 1 - c)).wait_recv()

        lane = lax.broadcasted_iota(jnp.int32, (1, T), 1)
        lane8 = lax.broadcasted_iota(jnp.int32, (T, T), 1)
        sub = lax.broadcasted_iota(jnp.int32, (T, T), 0)
        high = f32(4.0)

        def col_cap(k, slot):
            return jnp.where(lane + k * T < lens[slot, 0:1, :], high, f32(LOW))

        def row_cap(k, slot):
            return jnp.where(sub + k * T < lens[slot, 0:1, :], high, f32(LOW))

        def group(k, g):
            return units[k, pl.ds(2 * g, 2)].reshape(2 * T, units.shape[3])

        def against(k, g, h, js, keep):
            new = group(k, g)
            best = [[None, None], [None, None]]
            caps = [row_cap(k, 2 * g + q) for q in range(2)]
            for j in js:
                similar = lax.dot_general(new, group(j, h), (((1,), (1,)), ((), ())),
                                          preferred_element_type=f32)
                for w in range(2):
                    cap = col_cap(j, 2 * h + w)
                    for q in range(2):
                        part = similar[q * T:(q + 1) * T, w * T:(w + 1) * T]
                        m = jnp.minimum(part, cap)
                        best[q][w] = m if best[q][w] is None else jnp.maximum(best[q][w], m)
                        if keep(j):
                            n = jnp.max(jnp.minimum(part, caps[q]), axis=0, keepdims=True)
                            at_row = (2 * h + w) * slots + 2 * g + q
                            cols[j, pl.ds(at_row, 1), :] = jnp.maximum(cols[j, pl.ds(at_row, 1), :], n)
            table = rows[k]
            for q in range(2):
                for w in range(2):
                    top = jnp.max(best[q][w], axis=1, keepdims=True)
                    table = jnp.where(lane8 == (2 * g + q) * slots + 2 * h + w, top, table)
            rows[k] = table

        def share_out(k):
            for slot in others(k):
                to_side(k, slot).wait_recv()
                to_side(k, slot).start()

        share_out(0)
        for k in range(chunks):
            if k + 1 < chunks:
                share_out(k + 1)
            for d in range(chips):
                to_side(k, step(d) + 1 - c).wait_recv()

            @pl.loop(0, chips - 1, unroll=True)
            def _(i):
                g = jnp.where(c == 0, i, lax.rem(3 * i + 2, chips + 1))
                h = jnp.where(c == 0, i + 1, lax.rem(3 * i + 5, chips + 1))
                against(k, g, h, range(k + 1), lambda j: True)
                if k:
                    against(k, h, g, range(k), lambda j: True)

            @pl.loop(0, 2, unroll=True)
            def _(i):
                g = 2 * c + i
                against(k, g, g, range(k + 1), lambda j: j < k)

        pair = slots * slots
        total = jnp.zeros((pair, 1), f32)
        own_len = jnp.concatenate([lens[a] for a in range(slots)], axis=0)
        for k in range(chunks):
            best = jnp.maximum(rows[k].T[:pair], cols[k, :pair])
            ok = (lax.broadcasted_iota(jnp.int32, (pair, T), 1) + k * T < own_len) & (best > -3.5)
            total += jnp.sum(jnp.where(ok, best, f32(0.0)), axis=1, keepdims=True)
        share = total / own_len.astype(f32)
        place = lax.broadcasted_iota(jnp.int32, (pair, T), 0) % slots
        spread = jnp.where(lax.broadcasted_iota(jnp.int32, (pair, T), 1) == place, share, f32(0.0))
        res[c] = jnp.sum(spread.reshape(slots, slots, T), axis=1)
        for d in range(1, slots):
            copy(res.at[c], res.at[c], res_out.at[d], res_in.at[c], at(p, lax.rem(s + d, slots))).start()
        for k in range(chunks):
            hand_on(k).wait_send()
            for d in range(chips):
                to_side(k, step(d) + c).wait_send()
        tell(0, at(p, 2 * z + 1 - c)).wait_send()
        copy(res.at[1 - c], res.at[1 - c], res_out.at[0], res_in.at[1 - c], at(p, 2 * z + 1 - c)).wait_recv()

    @pl.when(jnp.logical_not(is_hub))
    def _():
        for k in range(chunks):
            straight(k).wait_send()
        for core in range(2):
            tell(core, at(p, 2 * hub_z + core)).wait_send()
        for core in range(2):
            copy(res.at[core], res.at[core], res_out.at[0], res_in.at[core],
                 at(p, 2 * hub_z + core)).wait_recv()

    whole = res[0] + res[1]
    first = lax.broadcasted_iota(jnp.int32, (slots, T), 0)
    second = lax.broadcasted_iota(jnp.int32, (slots, T), 1)
    row = jnp.sum(jnp.where(first == s, whole, f32(0.0)), axis=0, keepdims=True)
    prec_ref[...] = row[:, :slots]
    mine = ((first == s) | (second == s)) & (first != second)
    both = jnp.sum(jnp.where(mine, whole, f32(0.0)), axis=0, keepdims=True)
    util_ref[...] = jnp.sum(both, axis=1, keepdims=True) / f32(2 * (slots - 1))

    @pl.when(is_hub)
    def _():
        for d in range(1, slots):
            copy(res.at[c], res.at[c], res_out.at[d], res_in.at[c], at(p, lax.rem(s + d, slots))).wait_send()


def fused(slots, embeddings, lengths):
    length, width = embeddings.shape[1:]
    chunks = length // T
    dma = pltpu.SemaphoreType.DMA
    precision, utility = pl.pallas_call(
        functools.partial(kernel, slots // 2, slots),
        out_shape=(jax.ShapeDtypeStruct((1, slots), jnp.float32), jax.ShapeDtypeStruct((1, 1), jnp.float32)),
        in_specs=[pl.BlockSpec(memory_space=pltpu.SMEM), pl.BlockSpec(memory_space=pltpu.VMEM)],
        out_specs=(pl.BlockSpec(memory_space=pltpu.VMEM), pl.BlockSpec(memory_space=pltpu.VMEM)),
        scratch_shapes=[
            pltpu.VMEM((chunks, slots, T, width), jnp.bfloat16),
            pltpu.VMEM((chunks, T, width), jnp.bfloat16),
            pltpu.VMEM((slots, 8, T), jnp.int32),
            pltpu.VMEM((chunks, T, T), jnp.float32),
            pltpu.VMEM((chunks, slots * slots, T), jnp.float32),
            pltpu.VMEM((2, slots, T), jnp.float32),
            dma((slots, chunks)), dma((chunks,)), dma((slots,)), dma((2,)),
            dma((chunks,)), dma((slots, chunks)), dma((chunks,)), dma((2,)), dma((slots,)),
        ],
        compiler_params=pltpu.CompilerParams(collective_id=0, has_side_effects=True),
    )(lengths, embeddings)
    return precision, utility[:, 0]


def tile_pairs(own, own_len, other, other_len):
    similar = jnp.einsum("aie,bje->abij", own, other, preferred_element_type=jnp.float32)
    places = jnp.arange(own.shape[1], dtype=jnp.int32)
    own_ok = places[None, :] < own_len[:, None]
    other_ok = places[None, :] < other_len[:, None]
    masked = jnp.where(other_ok[None, :, None, :], similar, jnp.float32(-4.0))
    best_row = jnp.max(masked, axis=3)
    forward = jnp.sum(jnp.where(own_ok[:, None, :], best_row, jnp.float32(0.0)), axis=2)
    forward = forward / own_len[:, None].astype(jnp.float32)
    masked_col = jnp.where(own_ok[:, None, :, None], similar, jnp.float32(-4.0))
    best_col = jnp.max(masked_col, axis=2)
    backward = jnp.sum(jnp.where(other_ok[None, :, :], best_col, jnp.float32(0.0)), axis=2)
    backward = backward / other_len[None, :].astype(jnp.float32)
    return (forward, backward)


def body(embeddings, lengths):
    values = embeddings.astype(jnp.float32)
    unit = (values / jnp.sqrt(jnp.sum(values * values, axis=2, keepdims=True) + 1e-06)).astype(
        jnp.bfloat16
    )
    devices = lax.axis_size("sample")
    here = lax.axis_index("sample")
    per_dev = unit.shape[0]
    total = per_dev * devices
    base = here * per_dev
    piece = lax.all_gather(unit, "sample", axis=0, tiled=True)
    piece_len = lax.all_gather(lengths, "sample", axis=0, tiled=True)
    ahead, behind = tile_pairs(unit, lengths, piece, piece_len)
    own_index = base + jnp.arange(per_dev, dtype=jnp.int32)
    offdiag = jnp.arange(total, dtype=jnp.int32)[None, :] != own_index[:, None]
    utility = jnp.sum(jnp.where(offdiag, ahead + behind, jnp.float32(0.0)), axis=1)
    utility = utility / jnp.float32(2 * (total - 1))
    return (ahead, utility)


def solution(mesh):
    in_specs = (P(("prompt", "sample"), None, None), P(("prompt", "sample")))
    out_specs = (P(("prompt", "sample"), None), P(("prompt", "sample")))

    def run(embeddings, lengths):
        slots = mesh.shape["sample"]
        if mesh.shape["prompt"] == 4 and slots == 8 and embeddings.shape[0] == 1 and embeddings.shape[1] % T == 0:
            return fused(slots, embeddings, lengths)
        return body(embeddings, lengths)

    return jax.shard_map(run, mesh=mesh, in_specs=in_specs, out_specs=out_specs, check_vma=False)
```
